32 devices in a mesh: dp: 8 (over z, x), tensor: 4 (over y, core).
Axes of the slice: x: 2, y: 2, z: 4, core: 2. Of those that a mesh axis runs over, the one named last changes fastest.
Arguments:
- hidden_in: bfloat16 [4096, 2048], P(('dp', 'tensor')), may hold values from -6 to 6
- segment_ids: int32 [8, 512], P('dp'), may hold values from 0 to 3, never falling along the last dimension, each value on 1 to 256 neighbouring positions
- qkv_weight: bfloat16 [2, 2048, 3, 2048], P(None, 'dp', None, 'tensor'), may hold values from -0.125 to 0.125
- qkv_bias: bfloat16 [2, 3, 32, 64], P(None, None, 'tensor', 'dp'), may hold values from -3 to 3
- out_weight: bfloat16 [2, 2048, 2048], P(None, 'tensor', 'dp'), may hold values from -0.5 to 0.5
- gate_up_weight: bfloat16 [2, 2048, 2, 5632], P(None, 'dp', None, 'tensor'), may hold values from -0.125 to 0.125
- down_weight: bfloat16 [2, 5632, 2048], P(None, 'tensor', 'dp'), may hold values from -0.078125 to 0.078125
- norm_gain: bfloat16 [2, 2, 2048], P(None, None, 'dp'), may hold values from 0.5 to 1.5
- norm_bias: bfloat16 [2, 2, 2048], P(None, None, 'dp'), may hold values from -2 to 2
- cotangent: bfloat16 [4096, 2048], P(('dp', 'tensor')), may hold values from -6 to 6
Outputs:
- hidden_out: float32 [4096, 2048], P(('dp', 'tensor'))
- grad_in: float32 [4096, 2048], P(('dp', 'tensor'))
- grad_qkv_weight: float32 [2, 2048, 3, 2048], P(None, 'dp', None, 'tensor')
- grad_qkv_bias: float32 [2, 3, 32, 64], P(None, None, 'tensor', 'dp')
- grad_out_weight: float32 [2, 2048, 2048], P(None, 'tensor', 'dp')
- grad_gate_up_weight: float32 [2, 2048, 2, 5632], P(None, 'dp', None, 'tensor')
- grad_down_weight: float32 [2, 5632, 2048], P(None, 'tensor', 'dp')
- grad_norm_gain: float32 [2, 2, 2048], P(None, None, 'dp')
- grad_norm_bias: float32 [2, 2, 2048], P(None, None, 'dp')
The draws below stay inside these ranges and needn't reach their ends.
Inputs may be any that keep to these rules, and one draw needn't show every extreme that they name: `segment_ids`: segment numbers never fall along a packed sequence; each segment holds 1 to 256 positions, and some segment holds exactly 256.
All inputs are finite; a program needn't handle non-finite values.
Results may differ from the reference program's by a relative error of at most 0.025.
Values may be sent and summed in bfloat16 or wider, within the bound.
No kernel may reach another device: no remote copies, remote signals or barrier semaphores. Data moves between devices by JAX's collectives and lax.ppermute only.
A program may use at most 320 MiB of HBM per device.

```python
import math
import jax
import jax.numpy as jnp
import numpy as np
from jax import lax

D = 2048
HEADS = 32
HEAD_DIM = 64
FF = 5632
ROT = 16
LAYERS = 2
SEQ_LEN = 512
SEQS = 8
TOKENS = 4096


def spiked(result, key, source, target, shards_of, factor):
    def block_of(dim):
        return (jnp.arange(result.shape[dim]) // (result.shape[dim] // shards_of)).reshape((-1,) + (1,) * (result.ndim - 1 - dim))

    first = jax.random.permutation(key, shards_of)[block_of(target)]
    other_side = (block_of(target) + shards_of // 2) % shards_of
    return jnp.where((block_of(source) == first) | (block_of(source) == other_side), factor * result, result)


def block_scale(stream_key, dims, cuts, smallest, high):
    gain, own = 1.0, jax.random.fold_in(stream_key, 6)
    for axis_at, blocks in cuts:
        heights = jnp.exp(jax.random.uniform(jax.random.fold_in(own, axis_at), (blocks,), jnp.float32, smallest / len(cuts), high / len(cuts)))
        gain = gain * jnp.repeat(heights, dims[axis_at] // blocks).reshape([-1 if axis == axis_at else 1 for axis in range(len(dims))])
    return gain


def profile(number_of, total, bound, slope):
    loads = [(1 << 20) // math.isqrt(rank ** slope) + 1 for rank in range(2, number_of + 1)]
    surplus, holding = total - bound - (number_of - 1), [1] * (number_of - 1)
    while surplus > 0:
        free = [i for i in range(number_of - 1) if holding[i] < bound]
        whole, budget = sum([loads[i] for i in free]), surplus
        for i in free:
            extra = min(bound - holding[i], max(1, budget * loads[i] // whole), surplus)
            holding[i] = holding[i] + extra
            surplus = surplus - extra
    return np.array([bound] + holding)


def ragged(rng, number_of, total, limit, slope):
    if number_of == 2:
        one = jax.random.randint(rng, (), max(1, total - limit), min(limit, total - 1) + 1)
        return jnp.stack([one, total - one])
    tallies = jnp.asarray(profile(number_of, total, limit, slope), jnp.int32)
    couples = (number_of - 1) // 2
    source_of, sink = tallies[1:1 + 2 * couples:2], tallies[2:2 + 2 * couples:2]
    room = jnp.minimum(source_of - 1, limit - sink)
    shifted = jax.random.randint(jax.random.fold_in(rng, 1), (couples,), 0, 1 << 20) % (room + 1)
    tallies = tallies.at[1:1 + 2 * couples:2].set(source_of - shifted).at[2:2 + 2 * couples:2].set(sink + shifted)
    return tallies[jax.random.permutation(jax.random.fold_in(rng, 2), number_of)]


def gaussian(rng, shape, deviation, bound, split=(), kind=jnp.bfloat16):
    level = block_scale(rng, shape, split, -0.22, 0.18) if split else 1.0
    drawn = jax.random.normal(rng, shape, jnp.float32) * deviation * level
    return jnp.minimum(jnp.maximum(drawn, -bound), bound).astype(kind)


def gaussian_with(stream_key, dims, spread, limit, pieces, heavy, kind=jnp.bfloat16):
    entries = spread * jax.random.normal(stream_key, dims, jnp.float32)
    if pieces:
        entries = entries * block_scale(stream_key, dims, pieces, -0.22, 0.18)
    return jnp.clip(spiked(entries, jax.random.fold_in(stream_key, 3), *heavy), -limit, limit).astype(kind)


def setup_inputs(seed: int = 0) -> dict:
    streams_of = jax.random.split(jax.random.key(seed), 11)
    return {
        "hidden_in": gaussian(streams_of[0], (TOKENS, D), 1.0, 6.0, ((0, 32),)),
        "segment_ids": jax.vmap(lambda own: jnp.searchsorted(jnp.cumsum(ragged(own, 4, SEQ_LEN, SEQ_LEN // 2, 0)), jnp.arange(SEQ_LEN), side="right"))(jax.random.split(streams_of[1], SEQS)).reshape((SEQS, SEQ_LEN)).astype(jnp.int32),
        "qkv_weight": gaussian(streams_of[2], (LAYERS, D, 3, D), D ** -0.5, 0.125, ((1, 8), (3, 4))),
        "qkv_bias": gaussian(streams_of[3], (LAYERS, 3, HEADS, HEAD_DIM), 0.5, 3.0, ((2, 4), (3, 8))),
        "out_weight": gaussian(streams_of[4], (LAYERS, D, D), (D // 16) ** -0.5, 0.5, ((1, 4), (2, 8))),
        "gate_up_weight": gaussian(streams_of[5], (LAYERS, D, 2, FF), D ** -0.5, 0.125, ((1, 8), (3, 4))),
        "down_weight": gaussian(streams_of[6], (LAYERS, FF, D), FF ** -0.5, 0.078125, ((1, 4), (2, 8))),
        "norm_gain": jnp.clip(1.0 + 0.1 * jax.random.normal(streams_of[7], (LAYERS, 2, D), jnp.float32), 0.5, 1.5).astype(jnp.bfloat16),
        "norm_bias": gaussian(streams_of[8], (LAYERS, 2, D), 0.3, 2.0, ((2, 8),)),
        "cotangent": gaussian_with(streams_of[9], (TOKENS, D), 1.0, 6.0, ((0, 32),), (0, 1, 32, 2.75)),
    }


@jax.custom_vjp
def low(v):
    return lax.optimization_barrier(v.astype(jnp.bfloat16)).astype(jnp.float32)

@jax.custom_vjp
def low_back(v):
    return v

def low_keep(v):
    return (low(v), None)

def low_pass(kept, grad):
    return (grad,)

def back_keep(v):
    return (v, None)

def back_low(kept, grad):
    return (low(grad),)
low.defvjp(low_keep, low_pass)
low_back.defvjp(back_keep, back_low)
EPSILON = 1e-05
NEGATIVE = -1e+30
HIGHEST_PREC = lax.Precision.HIGHEST

def tables(segments):
    length = segments.shape[0]
    row_index = jnp.arange(length, dtype=jnp.int32)
    same_doc = segments[:, None] == segments[None, :]
    first_row = lax.optimization_barrier(jnp.min(jnp.where(same_doc, row_index[None, :], length), axis=1))
    positions = (row_index - first_row).astype(jnp.float32)
    frequency = jnp.power(10000.0, -jnp.arange(ROT // 2, dtype=jnp.float32) * (2.0 / ROT))
    angles = positions[:, None] * frequency[None, :]
    angles = jnp.concatenate([angles, angles], axis=1)
    allowed = same_doc & (row_index[:, None] >= row_index[None, :])
    return (jnp.cos(angles)[:, None, :], jnp.sin(angles)[:, None, :], allowed)

def rotate(heads_in, cos_table, sin_table):
    rot_part = heads_in[..., :ROT]
    half_rot = ROT // 2
    turned = jnp.concatenate([-rot_part[..., half_rot:], rot_part[..., :half_rot]], axis=-1)
    return jnp.concatenate([rot_part * cos_table + turned * sin_table, heads_in[..., ROT:]], axis=-1)

def layer_norm(rows, norm_gain, norm_shift):
    row_mean = lax.optimization_barrier(jnp.mean(rows, axis=1, keepdims=True))
    centred = rows - row_mean
    variance = lax.optimization_barrier(jnp.mean(centred * centred, axis=1, keepdims=True))
    return centred * lax.rsqrt(variance + EPSILON) * norm_gain + norm_shift

def attend_sequence(operands):
    projected, segments = operands
    cos_table, sin_table, allowed = tables(segments)
    queries = low(rotate(projected[:, 0], cos_table, sin_table))
    key_rows = low(rotate(projected[:, 1], cos_table, sin_table))
    val_rows = low(projected[:, 2])
    scores = jnp.einsum('qhd,khd->hqk', queries, key_rows, precision=HIGHEST_PREC) * HEAD_DIM ** (-0.5)
    scores = low_back(jnp.where(allowed[None], scores, NEGATIVE))
    log_total = jnp.log(lax.optimization_barrier(jnp.sum(jnp.exp(scores), axis=2, keepdims=True)))
    probs = low(jnp.exp(scores - log_total))
    return jnp.einsum('hqk,khd->qhd', probs, val_rows, precision=HIGHEST_PREC)

def forward(hidden, qkv_weight, qkv_bias, out_weight, gate_up_weight, down_weight, norm_gain, norm_bias, segment_ids):
    residual = hidden
    for layer_idx in range(LAYERS):
        normed = low(layer_norm(residual, norm_gain[layer_idx, 0], norm_bias[layer_idx, 0]))
        projected = jnp.dot(normed, qkv_weight[layer_idx].reshape(D, 3 * D), precision=HIGHEST_PREC)
        projected = projected + qkv_bias[layer_idx].reshape(3 * D)
        projected = low_back(projected).reshape(SEQS, SEQ_LEN, 3, HEADS, HEAD_DIM)
        mixed_rows = lax.map(jax.checkpoint(attend_sequence), (projected, segment_ids))
        mixed_rows = low(low_back(mixed_rows.reshape(TOKENS, D)))
        residual = residual + low_back(jnp.dot(mixed_rows, out_weight[layer_idx], precision=HIGHEST_PREC))
        normed = low(layer_norm(residual, norm_gain[layer_idx, 1], norm_bias[layer_idx, 1]))
        gate_up = jnp.dot(normed, gate_up_weight[layer_idx].reshape(D, 2 * FF), precision=HIGHEST_PREC)
        gate_up = low_back(gate_up).reshape(TOKENS, 2, FF)
        hidden_low = low(jax.nn.silu(gate_up[:, 0]) * gate_up[:, 1])
        residual = residual + low_back(jnp.dot(hidden_low, down_weight[layer_idx], precision=HIGHEST_PREC))
    return residual

def reference(hidden_in, segment_ids, qkv_weight, qkv_bias, out_weight, gate_up_weight, down_weight, norm_gain, norm_bias, cotangent):
    inputs = (hidden_in, qkv_weight, qkv_bias, out_weight, gate_up_weight, down_weight, norm_gain, norm_bias)
    floats = tuple((value_in.astype(jnp.float32) for value_in in inputs))

    def run_layers(*values):
        return forward(*values, segment_ids)
    output, pullback = jax.vjp(run_layers, *floats)
    grads = pullback(cotangent.astype(jnp.float32))
    return (output, grads[0], grads[1], grads[2], grads[3], grads[4], grads[5], grads[6], grads[7])
```

```python
import jax
import jax.numpy as jnp
from jax import lax
from jax.sharding import PartitionSpec as P

HEAD_DIM = 64
ROT = 16
EPSILON = 1e-05
NEGATIVE = -1e30
PAIR = 2
PAIR_MLP = True


f32 = jnp.float32
bf16 = jnp.bfloat16


def masks_of(count):
    masks = [PAIR, 6, 1]
    while 1 << len(masks) < count:
        masks.append(1 << len(masks))
    return masks


def slots_of(count):
    slots = [0]
    for mask in masks_of(count):
        slots = slots + [slot ^ mask for slot in slots]
    return slots


def trade(value, mask, axis="dp"):
    count = lax.axis_size(axis)
    return lax.ppermute(value, axis, [(i, i ^ mask) for i in range(count)])


def spread(first, axis):
    parts = [first]
    for mask in masks_of(lax.axis_size("dp"))[1:]:
        parts = parts + [trade(part, mask) for part in parts]
    return jnp.concatenate(parts, axis=axis)


def gather_whole(block, axis):
    return spread(jnp.concatenate([block, trade(block, PAIR)], axis=axis), axis)


def gather_half(mine, theirs, axis):
    return spread(jnp.concatenate([mine, trade(theirs, PAIR)], axis=axis), axis)


def fold(parts):
    for mask in reversed(masks_of(lax.axis_size("dp"))[1:]):
        half = len(parts) // 2
        got = [trade(part, mask) for part in parts[half:]]
        parts = [
            (a.astype(f32) + b.astype(f32)).astype(bf16) for a, b in zip(parts[:half], got)
        ]
    return parts[0]


def two(part, axis):
    half = part.shape[axis] // 2
    return lax.slice_in_dim(part, 0, half, axis=axis), lax.slice_in_dim(
        part, half, 2 * half, axis=axis
    )


def reduce_whole(parts, axis):
    keep, send = two(fold(parts), axis)
    return keep.astype(f32) + trade(send, PAIR).astype(f32)


def reduce_half(parts, axis):
    keep, send = two(fold(parts), axis)
    return keep, trade(send, PAIR)


def column_parts(array):
    count = lax.axis_size("dp") // 2
    width = array.shape[1] // count
    return [array[:, k * width : (k + 1) * width] for k in range(count)]


def relative(array, me):
    count = lax.axis_size("dp")
    width = array.shape[1] // count
    return jnp.concatenate(
        [
            lax.dynamic_slice_in_dim(array, (me ^ slot) * width, width, axis=1)
            for slot in slots_of(count)
        ],
        axis=1,
    )


def absolute(array, me):
    count = lax.axis_size("dp")
    width = array.shape[1] // count
    where = [0] * count
    for place, slot in enumerate(slots_of(count)):
        where[slot] = place
    table = jnp.asarray(where, dtype=jnp.int32)
    return jnp.concatenate(
        [
            lax.dynamic_slice_in_dim(array, table[me ^ block] * width, width, axis=1)
            for block in range(count)
        ],
        axis=1,
    )


def flip(array):
    count = lax.axis_size("dp")
    width = array.shape[1] // count
    return jnp.concatenate(
        [array[:, (r ^ 1) * width : ((r ^ 1) + 1) * width] for r in range(count)], axis=1
    )


def tables(segments):
    length = segments.shape[0]
    row_index = jnp.arange(length, dtype=jnp.int32)
    same_doc = segments[:, None] == segments[None, :]
    first_row = jnp.min(jnp.where(same_doc, row_index[None, :], length), axis=1)
    positions = (row_index - first_row).astype(f32)
    frequency = jnp.power(10000.0, -jnp.arange(ROT // 2, dtype=f32) * (2.0 / ROT))
    angles = positions[:, None] * frequency[None, :]
    angles = jnp.concatenate([angles, angles], axis=1)
    allowed = same_doc & (row_index[:, None] >= row_index[None, :])
    return (jnp.cos(angles)[:, None, :], jnp.sin(angles)[:, None, :], allowed)


def rotate(heads_in, cos_table, sin_table):
    rot_part = heads_in[..., :ROT]
    half_rot = ROT // 2
    turned = jnp.concatenate([-rot_part[..., half_rot:], rot_part[..., :half_rot]], axis=-1)
    return jnp.concatenate(
        [rot_part * cos_table + turned * sin_table, heads_in[..., ROT:]], axis=-1
    )


def rotate_back(grads_in, cos_table, sin_table):
    rot_part = grads_in[..., :ROT]
    half_rot = ROT // 2
    scaled = rot_part * sin_table
    turned = jnp.concatenate([scaled[..., half_rot:], -scaled[..., :half_rot]], axis=-1)
    return jnp.concatenate([rot_part * cos_table + turned, grads_in[..., ROT:]], axis=-1)


def layer_norm(rows, norm_gain, norm_shift):
    row_mean = jnp.mean(rows, axis=1, keepdims=True)
    centred = rows - row_mean
    variance = jnp.mean(centred * centred, axis=1, keepdims=True)
    inv_std = lax.rsqrt(variance + EPSILON)
    unit_rows = centred * inv_std
    return (unit_rows * norm_gain + norm_shift, unit_rows, inv_std)


def norm_back(grad_normed, unit_rows, inv_std, norm_gain):
    scaled = grad_normed * norm_gain
    centred = scaled - jnp.mean(scaled, axis=1, keepdims=True)
    grad_rows = inv_std * (
        centred - unit_rows * jnp.mean(scaled * unit_rows, axis=1, keepdims=True)
    )
    return (grad_rows, jnp.sum(grad_normed * unit_rows, axis=0), jnp.sum(grad_normed, axis=0))


def rows_of(rows, paired):
    if not paired:
        return lax.all_gather(rows, "tensor", axis=0, tiled=True)
    both = jnp.stack([rows, trade(flip(rows), PAIR)])
    full = lax.all_gather(both, "tensor", axis=1, tiled=True)
    return full.reshape(-1, rows.shape[1])


def sums_of(product, paired):
    if not paired:
        return lax.psum_scatter(
            product, "tensor", scatter_dimension=0, tiled=True
        ).astype(f32)
    half = product.shape[0] // 2
    other = lax.psum_scatter(product[half:], "tensor", scatter_dimension=0, tiled=True)
    own = lax.psum_scatter(product[:half], "tensor", scatter_dimension=0, tiled=True)
    return own.astype(f32) + trade(flip(other), PAIR).astype(f32)


def times(a, b):
    return jnp.dot(a, b, preferred_element_type=f32)


def times_t(a, b):
    return lax.dot_general(a, b, (((1,), (1,)), ((), ())), preferred_element_type=f32)


def t_times(a, b):
    return lax.dot_general(a, b, (((0,), (0,)), ((), ())), preferred_element_type=f32)


def attend_one(queries, key_rows, val_rows, allowed):
    scores = jnp.einsum(
        "qhd,khd->hqk", queries, key_rows, preferred_element_type=f32
    ) * HEAD_DIM ** (-0.5)
    scores = jnp.where(allowed[None], scores, NEGATIVE)
    log_total = jnp.log(jnp.sum(jnp.exp(scores), axis=2, keepdims=True))
    probs = jnp.exp(scores - log_total).astype(bf16)
    mixed_rows = jnp.einsum("hqk,khd->qhd", probs, val_rows, preferred_element_type=f32)
    return (mixed_rows, log_total)


def attend_back(queries, key_rows, val_rows, allowed, log_total, grad_out):
    scores = jnp.einsum(
        "qhd,khd->hqk", queries, key_rows, preferred_element_type=f32
    ) * HEAD_DIM ** (-0.5)
    scores = jnp.where(allowed[None], scores, NEGATIVE)
    probs = jnp.exp(scores - log_total)
    grad_probs = jnp.einsum("qhd,khd->hqk", grad_out, val_rows, preferred_element_type=f32)
    row_dot = jnp.sum(probs * grad_probs, axis=2, keepdims=True)
    grad_scores = (probs * (grad_probs - row_dot)).astype(bf16)
    grad_query = jnp.einsum(
        "hqk,khd->qhd", grad_scores, key_rows, preferred_element_type=f32
    ) * HEAD_DIM ** (-0.5)
    grad_key = jnp.einsum(
        "hqk,qhd->khd", grad_scores, queries, preferred_element_type=f32
    ) * HEAD_DIM ** (-0.5)
    grad_value = jnp.einsum(
        "hqk,qhd->khd", probs.astype(bf16), grad_out, preferred_element_type=f32
    )
    return (grad_query, grad_key, grad_value)


def shards(
    hidden_in,
    segment_ids,
    qkv_weight,
    qkv_bias,
    out_weight,
    gate_up_weight,
    down_weight,
    norm_gain,
    norm_bias,
    cotangent,
):
    layers = qkv_weight.shape[0]
    count = lax.axis_size("dp")
    me = lax.axis_index("dp")
    side = ((me >> 1) ^ (me >> 2)) & 1
    width = hidden_in.shape[1]
    length = segment_ids.shape[1]
    local_width = qkv_weight.shape[3]
    heads = qkv_bias.shape[2]
    head_width = local_width // heads
    hidden = gate_up_weight.shape[3]
    half_hidden = hidden // 2
    masks = masks_of(count)

    packed = jnp.concatenate(
        [norm_gain.reshape(-1), norm_bias.reshape(-1), qkv_bias.reshape(-1)]
    ).reshape(1, -1)
    for mask in masks:
        packed = jnp.concatenate([packed, trade(packed, mask)], axis=0)
    cut = norm_gain.size
    gains = packed[:, :cut].reshape((count,) + norm_gain.shape).transpose(1, 2, 0, 3)
    gains = gains.reshape(layers, 2, width).astype(f32)
    shifts = packed[:, cut : 2 * cut].reshape((count,) + norm_bias.shape).transpose(1, 2, 0, 3)
    shifts = shifts.reshape(layers, 2, width).astype(f32)
    places = [0] * count
    for place, slot in enumerate(slots_of(count)):
        places[slot] = place
    order = jnp.asarray(places, dtype=jnp.int32)[me ^ jnp.arange(count)]
    biases = jnp.take(packed[:, 2 * cut :], order, axis=0)
    biases = biases.reshape((count,) + qkv_bias.shape).transpose(1, 2, 3, 0, 4)
    biases = biases.reshape(layers, 3 * local_width).astype(f32)

    cos_table, sin_table, allowed = tables(segment_ids[0])
    residual = relative(hidden_in, me).astype(f32)
    grad_resid = relative(cotangent, me).astype(f32)

    weights = []
    for layer in range(layers):
        qkv_w = gather_whole(qkv_weight[layer].reshape(-1, 3 * local_width), 0)
        out_w = gather_whole(out_weight[layer], 1)
        gu = gate_up_weight[layer]
        down = down_weight[layer]
        if PAIR_MLP:
            mine = lax.dynamic_slice_in_dim(gu, side * half_hidden, half_hidden, axis=2)
            theirs = lax.dynamic_slice_in_dim(gu, (1 - side) * half_hidden, half_hidden, axis=2)
            gu_w = gather_half(mine.reshape(-1, hidden), theirs.reshape(-1, hidden), 0)
            mine = lax.dynamic_slice_in_dim(down, side * half_hidden, half_hidden, axis=0)
            theirs = lax.dynamic_slice_in_dim(down, (1 - side) * half_hidden, half_hidden, axis=0)
            down_w = gather_half(mine, theirs, 1)
        else:
            gu_w = gather_whole(gu.reshape(-1, 2 * hidden), 0)
            down_w = gather_whole(down, 1)
        weights.append((qkv_w, out_w, gu_w, down_w))

    kept = []
    for layer in range(layers):
        qkv_w, out_w, gu_w, down_w = weights[layer]
        normed, unit_one, inv_one = layer_norm(residual, gains[layer, 0], shifts[layer, 0])
        rows_one = rows_of(normed.astype(bf16), False)
        projected = times(rows_one, qkv_w) + biases[layer]
        projected = projected.reshape(length, 3, heads, head_width)
        queries = rotate(projected[:, 0], cos_table, sin_table).astype(bf16)
        key_rows = rotate(projected[:, 1], cos_table, sin_table).astype(bf16)
        val_rows = projected[:, 2].astype(bf16)
        mixed_rows, log_total = attend_one(queries, key_rows, val_rows, allowed)
        mixed_low = mixed_rows.reshape(length, local_width).astype(bf16)
        residual = residual + sums_of(times(mixed_low, out_w).astype(bf16), False)
        normed, unit_two, inv_two = layer_norm(residual, gains[layer, 1], shifts[layer, 1])
        rows_two = rows_of(normed.astype(bf16), PAIR_MLP)
        gate_up = times(rows_two, gu_w)
        mid = gate_up.shape[1] // 2
        hidden_low = (jax.nn.silu(gate_up[:, :mid]) * gate_up[:, mid:]).astype(bf16)
        residual = residual + sums_of(times(hidden_low, down_w).astype(bf16), PAIR_MLP)
        kept.append(
            (
                unit_one,
                inv_one,
                rows_one,
                queries,
                key_rows,
                val_rows,
                log_total,
                mixed_low,
                unit_two,
                inv_two,
                rows_two,
                gate_up,
                hidden_low,
            )
        )

    grads = [None] * layers
    small = []
    for layer in reversed(range(layers)):
        qkv_w, out_w, gu_w, down_w = weights[layer]
        (
            unit_one,
            inv_one,
            rows_one,
            queries,
            key_rows,
            val_rows,
            log_total,
            mixed_low,
            unit_two,
            inv_two,
            rows_two,
            gate_up,
            hidden_low,
        ) = kept[layer]
        grad_full = rows_of(grad_resid.astype(bf16), PAIR_MLP)
        down_parts = [t_times(hidden_low, part).astype(bf16) for part in column_parts(grad_full)]
        grad_hidden = times_t(grad_full, down_w)
        mid = gate_up.shape[1] // 2
        gate_part = gate_up[:, :mid]
        up_part = gate_up[:, mid:]
        sigmoid_gate = jax.nn.sigmoid(gate_part)
        grad_gate = grad_hidden * up_part * sigmoid_gate * (1.0 + gate_part * (1.0 - sigmoid_gate))
        grad_upper = grad_hidden * (gate_part * sigmoid_gate)
        grad_gu = jnp.concatenate([grad_gate, grad_upper], axis=1).astype(bf16)
        grad_norm_two = sums_of(times_t(grad_gu, gu_w).astype(bf16), PAIR_MLP)
        gu_parts = [t_times(part, grad_gu).astype(bf16) for part in column_parts(rows_two)]
        if PAIR_MLP:
            mine, other = reduce_half(down_parts, 1)
            low = jnp.where(side == 0, mine, other)
            high = jnp.where(side == 0, other, mine)
            grad_down = jnp.concatenate([low, high], axis=0).astype(f32)
            mine, other = reduce_half(gu_parts, 0)
            low = jnp.where(side == 0, mine, other).reshape(-1, 2, half_hidden)
            high = jnp.where(side == 0, other, mine).reshape(-1, 2, half_hidden)
            grad_up_w = jnp.concatenate([low, high], axis=2).astype(f32)
        else:
            grad_down = reduce_whole(down_parts, 1)
            grad_up_w = reduce_whole(gu_parts, 0).reshape(-1, 2, hidden)
        grad_x_two, gain_two, shift_two = norm_back(
            grad_norm_two, unit_two, inv_two, gains[layer, 1]
        )
        grad_resid = grad_resid + grad_x_two
        grad_full = rows_of(grad_resid.astype(bf16), False)
        grad_mixed = times_t(grad_full, out_w).astype(bf16)
        out_parts = [t_times(mixed_low, part).astype(bf16) for part in column_parts(grad_full)]
        grad_out_w = reduce_whole(out_parts, 1)
        grad_mixed = grad_mixed.reshape(length, heads, head_width)
        grad_query, grad_key, grad_value = attend_back(
            queries, key_rows, val_rows, allowed, log_total, grad_mixed
        )
        grad_query = rotate_back(grad_query, cos_table, sin_table)
        grad_key = rotate_back(grad_key, cos_table, sin_table)
        grad_qkv = jnp.stack([grad_query, grad_key, grad_value], axis=1).astype(bf16)
        grad_qkv = grad_qkv.reshape(length, 3 * local_width)
        grad_norm_one = sums_of(times_t(grad_qkv, qkv_w).astype(bf16), False)
        qkv_parts = [t_times(part, grad_qkv).astype(bf16) for part in column_parts(rows_one)]
        grad_qkv_w = reduce_whole(qkv_parts, 0).reshape(-1, 3, local_width)
        bias_sum = jnp.sum(grad_qkv, axis=0, dtype=f32)
        grad_x_one, gain_one, shift_one = norm_back(
            grad_norm_one, unit_one, inv_one, gains[layer, 0]
        )
        grad_resid = grad_resid + grad_x_one
        grads[layer] = (grad_qkv_w, grad_out_w, grad_up_w, grad_down)

        norms = jnp.stack([gain_one, gain_two, shift_one, shift_two])
        norms = norms.reshape(4, count, -1).transpose(1, 0, 2).reshape(count, -1)
        bias_sum = bias_sum.reshape(3, heads, count, -1).transpose(2, 0, 1, 3)
        back = me ^ jnp.asarray(slots_of(count), dtype=jnp.int32)
        bias_sum = jnp.take(bias_sum.reshape(count, -1), back, axis=0)
        row = jnp.concatenate([norms, bias_sum], axis=1)
        for mask in reversed(masks):
            half = row.shape[0] // 2
            row = row[:half] + trade(row[half:], mask)
        norms = row[0, : norms.shape[1]]
        bias_sum = row[0, norms.shape[0] :]
        step = 1
        while step < lax.axis_size("tensor"):
            norms = norms + trade(norms, step, "tensor")
            step *= 2
        norms = norms.reshape(2, 2, -1)
        small.append((norms[0], norms[1], bias_sum.reshape(3, heads, -1)))
    small = small[::-1]
    return (
        absolute(residual, me),
        absolute(grad_resid, me),
        jnp.stack([g[0] for g in grads]),
        jnp.stack([s[2] for s in small]),
        jnp.stack([g[1] for g in grads]),
        jnp.stack([g[2] for g in grads]),
        jnp.stack([g[3] for g in grads]),
        jnp.stack([s[0] for s in small]),
        jnp.stack([s[1] for s in small]),
    )


def solution(mesh):
    placed = (
        P(("dp", "tensor"), None),
        P("dp", None),
        P(None, "dp", None, "tensor"),
        P(None, None, "tensor", "dp"),
        P(None, "tensor", "dp"),
        P(None, "dp", None, "tensor"),
        P(None, "tensor", "dp"),
        P(None, None, "dp"),
        P(None, None, "dp"),
        P(("dp", "tensor"), None),
    )
    return jax.shard_map(
        shards,
        mesh=mesh,
        in_specs=placed,
        out_specs=(
            P(("dp", "tensor"), None),
            P(("dp", "tensor"), None),
            P(None, "dp", None, "tensor"),
            P(None, None, "tensor", "dp"),
            P(None, "tensor", "dp"),
            P(None, "dp", None, "tensor"),
            P(None, "tensor", "dp"),
            P(None, None, "dp"),
            P(None, None, "dp"),
        ),
        check_vma=False,
    )
```

```python
import jax
import jax.numpy as jnp
from jax import lax
from jax.sharding import PartitionSpec as P

HEAD_DIM = 64
ROT = 16
EPSILON = 1e-05
NEGATIVE = -1e30
PAIR = 2
FAR, NEAR = 2, 1
ROW_ORDER = (0, FAR, NEAR, FAR ^ NEAR)
PAIR_MLP = True


f32 = jnp.float32
bf16 = jnp.bfloat16


def rest_masks(count):
    masks = [6, 1]
    while 2 << len(masks) < count:
        masks.append(2 << len(masks))
    return masks


def rest_slots(count):
    slots = [0]
    for mask in rest_masks(count):
        slots = slots + [slot ^ mask for slot in slots]
    return slots


def trade(value, mask, name, axis="dp"):
    count = lax.axis_size(axis)
    with jax.named_scope(name):
        return lax.ppermute(value, axis, [(i, i ^ mask) for i in range(count)])


def choose(side, a, b):
    return jnp.where(side == 0, a, b), jnp.where(side == 0, b, a)


def spread(own, got, place, axis, name):
    low, high = choose(place, own, got)
    parts = [jnp.concatenate([low, high], axis=axis)]
    for step, mask in enumerate(rest_masks(lax.axis_size("dp"))):
        parts = parts + [
            trade(part, mask, f"{name}_s{step}{k}") for k, part in enumerate(parts)
        ]
    return jnp.concatenate(parts, axis=axis)


def gather_whole(block, place, axis, name):
    return spread(block, trade(block, PAIR, name + "_p"), place, axis, name)


def gather_half(mine, theirs, place, axis, name):
    return spread(mine, trade(theirs, PAIR, name + "_p"), place, axis, name)


def fold(parts, name):
    masks = rest_masks(lax.axis_size("dp"))
    for step in reversed(range(len(masks))):
        half = len(parts) // 2
        got = [
            trade(part, masks[step], f"{name}_s{step}{k}")
            for k, part in enumerate(parts[half:])
        ]
        parts = [
            (a.astype(f32) + b.astype(f32)).astype(bf16) for a, b in zip(parts[:half], got)
        ]
    return parts[0]


def two(part, axis):
    half = part.shape[axis] // 2
    return lax.slice_in_dim(part, 0, half, axis=axis), lax.slice_in_dim(
        part, half, 2 * half, axis=axis
    )


def reduce_whole(parts, place, axis, name):
    keep, send = choose(place, *two(fold(parts, name), axis))
    return keep.astype(f32) + trade(send, PAIR, name + "_p").astype(f32)


def reduce_half(parts, place, axis, name):
    keep, send = choose(place, *two(fold(parts, name), axis))
    return keep, trade(send, PAIR, name + "_p")


def column_parts(array):
    count = lax.axis_size("dp") // 2
    width = array.shape[1] // count
    return [array[:, k * width : (k + 1) * width] for k in range(count)]


def relative(array, me):
    count = lax.axis_size("dp")
    width = array.shape[1] // count
    return jnp.concatenate(
        [
            lax.dynamic_slice_in_dim(
                array, (((me ^ slot) & ~PAIR) | (PAIR * q)) * width, width, axis=1
            )
            for slot in rest_slots(count)
            for q in (0, 1)
        ],
        axis=1,
    )


def places_of(count):
    where = [0] * count
    for k, slot in enumerate(rest_slots(count)):
        where[slot & ~PAIR] = 2 * k
    return jnp.asarray(where, dtype=jnp.int32)


def place_of_block(me, block, table):
    return table[(me ^ block) & ~PAIR] + ((block // PAIR) & 1)


def absolute(array, me):
    count = lax.axis_size("dp")
    width = array.shape[1] // count
    table = places_of(count)
    return jnp.concatenate(
        [
            lax.dynamic_slice_in_dim(
                array, place_of_block(me, block, table) * width, width, axis=1
            )
            for block in range(count)
        ],
        axis=1,
    )


def tables(segments, seat):
    length = segments.shape[0]
    block = length // 4
    row_index = jnp.concatenate(
        [(seat ^ r) * block + jnp.arange(block, dtype=jnp.int32) for r in ROW_ORDER]
    )
    segments = jnp.concatenate(
        [lax.dynamic_slice_in_dim(segments, (seat ^ r) * block, block) for r in ROW_ORDER]
    )
    same_doc = segments[:, None] == segments[None, :]
    first_row = jnp.min(jnp.where(same_doc, row_index[None, :], length), axis=1)
    positions = (row_index - first_row).astype(f32)
    frequency = jnp.power(10000.0, -jnp.arange(ROT // 2, dtype=f32) * (2.0 / ROT))
    angles = positions[:, None] * frequency[None, :]
    angles = jnp.concatenate([angles, angles], axis=1)
    allowed = same_doc & (row_index[:, None] >= row_index[None, :])
    return (jnp.cos(angles)[:, None, :], jnp.sin(angles)[:, None, :], allowed)


def rotate(heads_in, cos_table, sin_table):
    rot_part = heads_in[..., :ROT]
    half_rot = ROT // 2
    turned = jnp.concatenate([-rot_part[..., half_rot:], rot_part[..., :half_rot]], axis=-1)
    return jnp.concatenate(
        [rot_part * cos_table + turned * sin_table, heads_in[..., ROT:]], axis=-1
    )


def rotate_back(grads_in, cos_table, sin_table):
    rot_part = grads_in[..., :ROT]
    half_rot = ROT // 2
    scaled = rot_part * sin_table
    turned = jnp.concatenate([scaled[..., half_rot:], -scaled[..., :half_rot]], axis=-1)
    return jnp.concatenate([rot_part * cos_table + turned, grads_in[..., ROT:]], axis=-1)


def layer_norm(rows, norm_gain, norm_shift):
    row_mean = jnp.mean(rows, axis=1, keepdims=True)
    centred = rows - row_mean
    variance = jnp.mean(centred * centred, axis=1, keepdims=True)
    inv_std = lax.rsqrt(variance + EPSILON)
    unit_rows = centred * inv_std
    return (unit_rows * norm_gain + norm_shift, unit_rows, inv_std)


def norm_back(grad_normed, unit_rows, inv_std, norm_gain):
    scaled = grad_normed * norm_gain
    centred = scaled - jnp.mean(scaled, axis=1, keepdims=True)
    grad_rows = inv_std * (
        centred - unit_rows * jnp.mean(scaled * unit_rows, axis=1, keepdims=True)
    )
    return (grad_rows, jnp.sum(grad_normed * unit_rows, axis=0), jnp.sum(grad_normed, axis=0))


def rows_of(rows, paired, name):
    far = trade(rows, FAR, name + "_y", "tensor")
    if not paired:
        return jnp.concatenate(
            [
                rows,
                far,
                trade(rows, NEAR, name + "_c0", "tensor"),
                trade(far, NEAR, name + "_c1", "tensor"),
            ]
        )
    pair = trade(rows, PAIR, name + "_z")
    half = rows.shape[0] // 2
    both = jnp.concatenate(
        [
            trade(pair[:half], FAR, name + "_zy", "tensor"),
            trade(far[half:], PAIR, name + "_yz"),
        ]
    )
    mine = [rows, far, pair, both]
    return jnp.concatenate(
        mine + [trade(part, NEAR, f"{name}_c{k}", "tensor") for k, part in enumerate(mine)]
    )


def sums_of(inputs, matrix, dot, paired, name):
    half = inputs.shape[0] // 2
    send = dot(inputs[half:], matrix).astype(bf16)
    got = trade(send, NEAR, name + "_c", "tensor")
    keep = dot(inputs[:half], matrix)
    if not paired:
        rows = half // 2
        send = (keep[rows:] + got[rows:].astype(f32)).astype(bf16)
        last = trade(send, FAR, name + "_y", "tensor")
        return keep[:rows] + got[:rows].astype(f32) + last.astype(f32)
    rows = half // 4
    wide = keep.shape[1] // 2

    def block(k, low):
        where = (slice(k * rows, (k + 1) * rows), slice(0, wide) if low else slice(wide, None))
        return keep[where] + got[where].astype(f32)

    send = jnp.concatenate([block(1, True), block(3, True)]).astype(bf16)
    low = trade(send, FAR, name + "_y", "tensor")
    send = jnp.concatenate([block(2, False), block(3, False)]).astype(bf16)
    high = trade(send, PAIR, name + "_z")
    send = (block(2, True) + low[rows:].astype(f32)).astype(bf16)
    last_low = trade(send, PAIR, name + "_yz")
    send = (block(1, False) + high[rows:].astype(f32)).astype(bf16)
    last_high = trade(send, FAR, name + "_zy", "tensor")
    return jnp.concatenate(
        [
            block(0, True) + low[:rows].astype(f32) + last_low.astype(f32),
            block(0, False) + high[:rows].astype(f32) + last_high.astype(f32),
        ],
        axis=1,
    )


def times(a, b):
    return jnp.dot(a, b, preferred_element_type=f32)


def times_t(a, b):
    return lax.dot_general(a, b, (((1,), (1,)), ((), ())), preferred_element_type=f32)


def t_times(a, b):
    return lax.dot_general(a, b, (((0,), (0,)), ((), ())), preferred_element_type=f32)


def attend_one(queries, key_rows, val_rows, allowed):
    scores = jnp.einsum(
        "qhd,khd->hqk", queries, key_rows, preferred_element_type=f32
    ) * HEAD_DIM ** (-0.5)
    scores = jnp.where(allowed[None], scores, NEGATIVE)
    log_total = jnp.log(jnp.sum(jnp.exp(scores), axis=2, keepdims=True))
    probs = jnp.exp(scores - log_total).astype(bf16)
    mixed_rows = jnp.einsum("hqk,khd->qhd", probs, val_rows, preferred_element_type=f32)
    return (mixed_rows, log_total)


def attend_back(queries, key_rows, val_rows, allowed, log_total, grad_out):
    scores = jnp.einsum(
        "qhd,khd->hqk", queries, key_rows, preferred_element_type=f32
    ) * HEAD_DIM ** (-0.5)
    scores = jnp.where(allowed[None], scores, NEGATIVE)
    probs = jnp.exp(scores - log_total)
    grad_probs = jnp.einsum("qhd,khd->hqk", grad_out, val_rows, preferred_element_type=f32)
    row_dot = jnp.sum(probs * grad_probs, axis=2, keepdims=True)
    grad_scores = (probs * (grad_probs - row_dot)).astype(bf16)
    grad_query = jnp.einsum(
        "hqk,khd->qhd", grad_scores, key_rows, preferred_element_type=f32
    ) * HEAD_DIM ** (-0.5)
    grad_key = jnp.einsum(
        "hqk,qhd->khd", grad_scores, queries, preferred_element_type=f32
    ) * HEAD_DIM ** (-0.5)
    grad_value = jnp.einsum(
        "hqk,qhd->khd", probs.astype(bf16), grad_out, preferred_element_type=f32
    )
    return (grad_query, grad_key, grad_value)


def shards(
    hidden_in,
    segment_ids,
    qkv_weight,
    qkv_bias,
    out_weight,
    gate_up_weight,
    down_weight,
    norm_gain,
    norm_bias,
    cotangent,
):
    layers = qkv_weight.shape[0]
    count = lax.axis_size("dp")
    me = lax.axis_index("dp")
    side = ((me >> 1) ^ (me >> 2)) & 1
    width = hidden_in.shape[1]
    length = segment_ids.shape[1]
    local_width = qkv_weight.shape[3]
    heads = qkv_bias.shape[2]
    head_width = local_width // heads
    hidden = gate_up_weight.shape[3]
    half_hidden = hidden // 2
    masks = [PAIR] + rest_masks(count)
    place = (me >> 1) & 1
    seat = lax.axis_index("tensor")

    packed = jnp.concatenate(
        [norm_gain.reshape(-1), norm_bias.reshape(-1), qkv_bias.reshape(-1)]
    ).reshape(1, -1)
    low, high = choose(place, packed, trade(packed, PAIR, "small_p"))
    packed = jnp.concatenate([low, high], axis=0)
    for step, mask in enumerate(masks[1:]):
        packed = jnp.concatenate([packed, trade(packed, mask, f"small_s{step}")], axis=0)
    cut = norm_gain.size
    gains = packed[:, :cut].reshape((count,) + norm_gain.shape).transpose(1, 2, 0, 3)
    gains = gains.reshape(layers, 2, width).astype(f32)
    shifts = packed[:, cut : 2 * cut].reshape((count,) + norm_bias.shape).transpose(1, 2, 0, 3)
    shifts = shifts.reshape(layers, 2, width).astype(f32)
    order = place_of_block(me, jnp.arange(count), places_of(count))
    biases = jnp.take(packed[:, 2 * cut :], order, axis=0)
    biases = biases.reshape((count,) + qkv_bias.shape).transpose(1, 2, 3, 0, 4)
    biases = biases.reshape(layers, 3 * local_width).astype(f32)

    cos_table, sin_table, allowed = tables(segment_ids[0], seat)
    residual = relative(hidden_in, me).astype(f32)
    grad_resid = relative(cotangent, me).astype(f32)

    weights = []
    for layer in range(layers):
        tag = f"w{layer}"
        if layer == 0:
            qkv_w = jnp.concatenate(
                [
                    gather_whole(qkv_weight[layer, :, k], place, 0, f"{tag}q{k}")
                    for k in range(3)
                ],
                axis=1,
            )
        else:
            qkv_w = gather_whole(
                qkv_weight[layer].reshape(-1, 3 * local_width), place, 0, tag + "q"
            )
        out_w = gather_whole(out_weight[layer], place, 1, tag + "o")
        gu = gate_up_weight[layer]
        down = down_weight[layer]
        if PAIR_MLP:
            low, high = gu[:, :, :half_hidden], gu[:, :, half_hidden:]
            low, high = low.reshape(-1, hidden), high.reshape(-1, hidden)
            mine, theirs = choose(side, low, high)
            gu_w = gather_half(mine, theirs, place, 0, tag + "g")
            mine, theirs = choose(side, *two(down, 0))
            down_w = gather_half(mine, theirs, place, 1, tag + "d")
        else:
            gu_w = gather_whole(gu.reshape(-1, 2 * hidden), place, 0, tag + "g")
            down_w = gather_whole(down, place, 1, tag + "d")
        weights.append((qkv_w, out_w, gu_w, down_w))

    kept = []
    for layer in range(layers):
        qkv_w, out_w, gu_w, down_w = weights[layer]
        normed, unit_one, inv_one = layer_norm(residual, gains[layer, 0], shifts[layer, 0])
        rows_one = rows_of(normed.astype(bf16), False, f"f{layer}a")
        projected = times(rows_one, qkv_w) + biases[layer]
        projected = projected.reshape(length, 3, heads, head_width)
        queries = rotate(projected[:, 0], cos_table, sin_table).astype(bf16)
        key_rows = rotate(projected[:, 1], cos_table, sin_table).astype(bf16)
        val_rows = projected[:, 2].astype(bf16)
        mixed_rows, log_total = attend_one(queries, key_rows, val_rows, allowed)
        mixed_low = mixed_rows.reshape(length, local_width).astype(bf16)
        residual = residual + sums_of(mixed_low, out_w, times, False, f"f{layer}b")
        normed, unit_two, inv_two = layer_norm(residual, gains[layer, 1], shifts[layer, 1])
        rows_two = rows_of(normed.astype(bf16), PAIR_MLP, f"f{layer}c")
        gate_up = times(rows_two, gu_w)
        mid = gate_up.shape[1] // 2
        hidden_low = (jax.nn.silu(gate_up[:, :mid]) * gate_up[:, mid:]).astype(bf16)
        residual = residual + sums_of(hidden_low, down_w, times, PAIR_MLP, f"f{layer}d")
        kept.append(
            (
                unit_one,
                inv_one,
                rows_one,
                queries,
                key_rows,
                val_rows,
                log_total,
                mixed_low,
                unit_two,
                inv_two,
                rows_two,
                gate_up,
                hidden_low,
            )
        )

    grads = [None] * layers
    small = []
    for layer in reversed(range(layers)):
        qkv_w, out_w, gu_w, down_w = weights[layer]
        (
            unit_one,
            inv_one,
            rows_one,
            queries,
            key_rows,
            val_rows,
            log_total,
            mixed_low,
            unit_two,
            inv_two,
            rows_two,
            gate_up,
            hidden_low,
        ) = kept[layer]
        grad_full = rows_of(grad_resid.astype(bf16), PAIR_MLP, f"b{layer}a")
        down_parts = [t_times(hidden_low, part).astype(bf16) for part in column_parts(grad_full)]
        grad_hidden = times_t(grad_full, down_w)
        mid = gate_up.shape[1] // 2
        gate_part = gate_up[:, :mid]
        up_part = gate_up[:, mid:]
        sigmoid_gate = jax.nn.sigmoid(gate_part)
        grad_gate = grad_hidden * up_part * sigmoid_gate * (1.0 + gate_part * (1.0 - sigmoid_gate))
        grad_upper = grad_hidden * (gate_part * sigmoid_gate)
        grad_gu = jnp.concatenate([grad_gate, grad_upper], axis=1).astype(bf16)
        grad_norm_two = sums_of(grad_gu, gu_w, times_t, PAIR_MLP, f"b{layer}b")
        gu_parts = [t_times(part, grad_gu).astype(bf16) for part in column_parts(rows_two)]
        if PAIR_MLP:
            mine, other = reduce_half(down_parts, place, 1, f"g{layer}d")
            low = jnp.where(side == 0, mine, other)
            high = jnp.where(side == 0, other, mine)
            grad_down = jnp.concatenate([low, high], axis=0).astype(f32)
            mine, other = reduce_half(gu_parts, place, 0, f"g{layer}g")
            low = jnp.where(side == 0, mine, other).reshape(-1, 2, half_hidden)
            high = jnp.where(side == 0, other, mine).reshape(-1, 2, half_hidden)
            grad_up_w = jnp.concatenate([low, high], axis=2).astype(f32)
        else:
            grad_down = reduce_whole(down_parts, place, 1, f"g{layer}d")
            grad_up_w = reduce_whole(gu_parts, place, 0, f"g{layer}g").reshape(-1, 2, hidden)
        grad_x_two, gain_two, shift_two = norm_back(
            grad_norm_two, unit_two, inv_two, gains[layer, 1]
        )
        grad_resid = grad_resid + grad_x_two
        grad_full = rows_of(grad_resid.astype(bf16), False, f"b{layer}c")
        grad_mixed = times_t(grad_full, out_w).astype(bf16)
        out_parts = [t_times(mixed_low, part).astype(bf16) for part in column_parts(grad_full)]
        grad_out_w = reduce_whole(out_parts, place, 1, f"g{layer}o")
        grad_mixed = grad_mixed.reshape(length, heads, head_width)
        grad_query, grad_key, grad_value = attend_back(
            queries, key_rows, val_rows, allowed, log_total, grad_mixed
        )
        grad_query = rotate_back(grad_query, cos_table, sin_table)
        grad_key = rotate_back(grad_key, cos_table, sin_table)
        grad_qkv = jnp.stack([grad_query, grad_key, grad_value], axis=1).astype(bf16)
        grad_qkv = grad_qkv.reshape(length, 3 * local_width)
        grad_norm_one = sums_of(grad_qkv, qkv_w, times_t, False, f"b{layer}d")
        qkv_parts = [t_times(part, grad_qkv).astype(bf16) for part in column_parts(rows_one)]
        grad_qkv_w = reduce_whole(qkv_parts, place, 0, f"g{layer}q").reshape(-1, 3, local_width)
        bias_sum = jnp.sum(grad_qkv, axis=0, dtype=f32)
        grad_x_one, gain_one, shift_one = norm_back(
            grad_norm_one, unit_one, inv_one, gains[layer, 0]
        )
        grad_resid = grad_resid + grad_x_one
        grads[layer] = (grad_qkv_w, grad_out_w, grad_up_w, grad_down)

        norms = jnp.stack([gain_one, gain_two, shift_one, shift_two])
        norms = norms.reshape(4, count, -1).transpose(1, 0, 2).reshape(count, -1)
        bias_sum = bias_sum.reshape(3, heads, count, -1).transpose(2, 0, 1, 3)
        slots = jnp.asarray(rest_slots(count), dtype=jnp.int32)
        back = ((me ^ slots) & ~PAIR)[:, None] | jnp.asarray([[0, PAIR]], dtype=jnp.int32)
        bias_sum = jnp.take(bias_sum.reshape(count, -1), back.reshape(-1), axis=0)
        row = jnp.concatenate([norms, bias_sum], axis=1)
        for step in reversed(range(1, len(masks))):
            half = row.shape[0] // 2
            row = row[:half] + trade(row[half:], masks[step], f"n{layer}_s{step}")
        keep, send = choose(place, row[:1], row[1:])
        row = keep + trade(send, PAIR, f"n{layer}_p")
        bias_sum = row[0, norms.shape[1] :]
        norms = row[:, : norms.shape[1]]
        for mask in (FAR, NEAR):
            norms = norms + trade(norms, mask, f"n{layer}_t{mask}", "tensor")
        norms = norms.reshape(2, 2, -1)
        small.append((norms[0], norms[1], bias_sum.reshape(3, heads, -1)))
    small = small[::-1]
    return (
        absolute(residual, me),
        absolute(grad_resid, me),
        jnp.stack([g[0] for g in grads]),
        jnp.stack([s[2] for s in small]),
        jnp.stack([g[1] for g in grads]),
        jnp.stack([g[2] for g in grads]),
        jnp.stack([g[3] for g in grads]),
        jnp.stack([s[0] for s in small]),
        jnp.stack([s[1] for s in small]),
    )


def solution(mesh):
    placed = (
        P(("dp", "tensor"), None),
        P("dp", None),
        P(None, "dp", None, "tensor"),
        P(None, None, "tensor", "dp"),
        P(None, "tensor", "dp"),
        P(None, "dp", None, "tensor"),
        P(None, "tensor", "dp"),
        P(None, None, "dp"),
        P(None, None, "dp"),
        P(("dp", "tensor"), None),
    )
    return jax.shard_map(
        shards,
        mesh=mesh,
        in_specs=placed,
        out_specs=(
            P(("dp", "tensor"), None),
            P(("dp", "tensor"), None),
            P(None, "dp", None, "tensor"),
            P(None, None, "tensor", "dp"),
            P(None, "tensor", "dp"),
            P(None, "dp", None, "tensor"),
            P(None, "tensor", "dp"),
            P(None, None, "dp"),
            P(None, None, "dp"),
        ),
        check_vma=False,
    )
```
